32 devices in a mesh: dp: 8 (over y, x, core), dap: 4 (over z).
Axes of the slice: x: 2, y: 2, z: 4, core: 2. Of those that a mesh axis runs over, the one named last changes fastest.
Arguments:
- pair_act: bfloat16 [8, 128, 128, 128], P('dp', 'dap'), may hold values from -6 to 6
- pair_cot: bfloat16 [8, 128, 128, 128], P('dp', 'dap'), may hold values from -6 to 6
- in_gain: float32 [128], replicated, may hold values from 0.25 to 1.75
- in_bias: float32 [128], replicated, may hold values from -3 to 3
- proj_weight: bfloat16 [128, 512], replicated, may hold values from -0.5 to 0.5
- gate_weight: bfloat16 [128, 128], replicated, may hold values from -0.5 to 0.5
- out_gain: float32 [128], replicated, may hold values from 0.25 to 1.75
- out_bias: float32 [128], replicated, may hold values from -3 to 3
- out_weight: bfloat16 [128, 128], replicated, may hold values from -0.5 to 0.5
Outputs:
- update: bfloat16 [8, 128, 128, 128], P('dp', 'dap')
- pair_grad: bfloat16 [8, 128, 128, 128], P('dp', 'dap')
- proj_grad: float32 [128, 512], replicated
- gate_grad: float32 [128, 128], replicated
- out_grad: float32 [128, 128], replicated
- in_norm_grad: float32 [2, 128], replicated
- out_norm_grad: float32 [2, 128], replicated
The draws below stay inside these ranges and needn't reach their ends.
All inputs are finite; a program needn't handle non-finite values.
Results may differ from the reference program's by a relative error of at most 0.0084.
Values may be sent and summed in bfloat16 or wider, within the bound.
A program may use at most 64 MiB of HBM per device.

```python
import jax
import jax.numpy as jnp
from jax import lax

C = 128
CH = 128
N = 128
CROPS = 8


def shard_levels(key, shape, cuts, smallest, high):
    def one(position, shards_of):
        draws = jax.random.uniform(jax.random.fold_in(jax.random.fold_in(key, 6), position), (shards_of,), jnp.float32, smallest / len(cuts), high / len(cuts))
        return jnp.repeat(jnp.exp(draws), shape[position] // shards_of).reshape((-1,) + (1,) * (len(shape) - position - 1))

    loudness = one(*cuts[0])
    for cut in cuts[1:]:
        loudness = loudness * one(*cut)
    return loudness


def scatter_about(key, shape, deviation, reach, shards=(), dtype=jnp.bfloat16):
    drawn = jax.random.normal(key, shape, jnp.float32) * deviation
    if len(shards) > 0:
        drawn = shard_levels(key, shape, shards, -0.22, 0.18) * drawn
    return jnp.clip(drawn, min=-reach, max=reach).astype(dtype)


def setup_inputs(seed: int = 0) -> dict:
    key_of = jax.random.split(jax.random.key(seed), 10)
    pair_act = scatter_about(key_of[0], (CROPS, N, N, C), 1.0, 6.0, ((0, 8), (1, 4)))
    pair_cot = scatter_about(key_of[1], (CROPS, N, N, C), 1.0, 6.0, ((0, 8), (1, 4)))
    in_gain = jnp.clip(1.0 + 0.15 * jax.random.normal(key_of[2], (C,), jnp.float32), 0.25, 1.75)
    in_bias = scatter_about(key_of[3], (C,), 0.3, 3.0, (), jnp.float32)
    proj_weight = scatter_about(key_of[4], (C, 4 * CH), C ** -0.5, 0.5)
    gate_weight = scatter_about(key_of[5], (C, C), C ** -0.5, 0.5)
    out_gain = jnp.clip(1.0 + 0.15 * jax.random.normal(key_of[6], (CH,), jnp.float32), 0.25, 1.75)
    out_bias = scatter_about(key_of[7], (CH,), 0.3, 3.0, (), jnp.float32)
    out_weight = scatter_about(key_of[8], (CH, C), CH ** -0.5, 0.5)
    return dict(pair_act=pair_act, pair_cot=pair_cot, in_gain=in_gain, in_bias=in_bias, proj_weight=proj_weight, gate_weight=gate_weight, out_gain=out_gain, out_bias=out_bias, out_weight=out_weight)


epsilon = 1e-05

def norm_rows(values, along):
    row_mean = lax.optimization_barrier(jnp.mean(values, axis=along, keepdims=True))
    centred = values - row_mean
    row_var = lax.optimization_barrier(jnp.mean(centred * centred, axis=along, keepdims=True))
    inv_std = lax.rsqrt(row_var + epsilon)
    return (centred * inv_std, inv_std)

def norm_back(grad_hat, x_hat, inv_std, along):
    first = lax.optimization_barrier(jnp.mean(grad_hat, axis=along, keepdims=True))
    second = lax.optimization_barrier(jnp.mean(grad_hat * x_hat, axis=along, keepdims=True))
    return (grad_hat - first - x_hat * second) * inv_std

def reference(pair_act, pair_cot, in_gain, in_bias, proj_weight, gate_weight, out_gain, out_bias, out_weight):
    f32 = jnp.float32
    bf16 = jnp.bfloat16

    def one_crop(operands):
        pair_one, cot_one = operands
        flat_act = pair_one.reshape(N * N, C).astype(f32)
        in_hat, in_inv = norm_rows(flat_act, 1)
        normed = (in_hat * in_gain + in_bias).astype(bf16)
        projected = jnp.dot(normed, proj_weight, preferred_element_type=f32)
        pre_ag = projected[:, 0:CH]
        pre_ap = projected[:, CH:2 * CH]
        pre_bg = projected[:, 2 * CH:3 * CH]
        pre_bp = projected[:, 3 * CH:4 * CH]
        sig_a = jax.nn.sigmoid(pre_ag)
        sig_b = jax.nn.sigmoid(pre_bg)
        left_act = (sig_a * pre_ap).astype(bf16).reshape(N, N, CH)
        right_act = (sig_b * pre_bp).astype(bf16).reshape(N, N, CH)
        tri_out = jnp.einsum('ikh,jkh->ijh', left_act.astype(f32), right_act.astype(f32)).astype(bf16)
        tri_hat, tri_inv = norm_rows(tri_out.reshape(N * N, CH).astype(f32), 1)
        tri_norm = (tri_hat * out_gain + out_bias).astype(bf16)
        gate_val = jax.nn.sigmoid(jnp.dot(normed, gate_weight, preferred_element_type=f32))
        mixed = jnp.dot(tri_norm, out_weight, preferred_element_type=f32)
        update = (gate_val * mixed).astype(bf16)
        cot_flat = cot_one.reshape(N * N, C).astype(f32)
        d_mixed = (cot_flat * gate_val).astype(bf16)
        d_gate = (cot_flat * mixed * gate_val * (1.0 - gate_val)).astype(bf16)
        out_part = jnp.dot(tri_norm.T, d_mixed, preferred_element_type=f32)
        gate_part = jnp.dot(normed.T, d_gate, preferred_element_type=f32)
        d_norm_out = jnp.dot(d_mixed, out_weight.T, preferred_element_type=f32)
        out_norm_part = jnp.stack([lax.optimization_barrier(jnp.sum(d_norm_out * tri_hat, axis=0)), lax.optimization_barrier(jnp.sum(d_norm_out, axis=0))])
        d_tri = norm_back(d_norm_out * out_gain, tri_hat, tri_inv, 1).astype(bf16).reshape(N, N, CH)
        d_left = jnp.einsum('ijh,jkh->ikh', d_tri.astype(f32), right_act.astype(f32)).astype(bf16)
        d_right = jnp.einsum('ijh,ikh->jkh', d_tri.astype(f32), left_act.astype(f32)).astype(bf16)
        left_grad = d_left.reshape(N * N, CH).astype(f32)
        right_grad = d_right.reshape(N * N, CH).astype(f32)
        d_proj = jnp.concatenate([left_grad * pre_ap * sig_a * (1.0 - sig_a), left_grad * sig_a, right_grad * pre_bp * sig_b * (1.0 - sig_b), right_grad * sig_b], axis=1).astype(bf16)
        proj_part = jnp.dot(normed.T, d_proj, preferred_element_type=f32)
        d_normed = jnp.dot(d_proj, proj_weight.T, preferred_element_type=f32) + jnp.dot(d_gate, gate_weight.T, preferred_element_type=f32)
        in_norm_part = jnp.stack([lax.optimization_barrier(jnp.sum(d_normed * in_hat, axis=0)), lax.optimization_barrier(jnp.sum(d_normed, axis=0))])
        pair_grad = norm_back(d_normed * in_gain, in_hat, in_inv, 1).astype(bf16)
        return (update.reshape(N, N, C), pair_grad.reshape(N, N, C), proj_part, gate_part, out_part, in_norm_part, out_norm_part)
    results = lax.map(one_crop, (pair_act, pair_cot))
    update, pair_grad, proj_all, gate_all, out_all, in_all, outn_all = results
    scale = 1.0 / N
    return (update, pair_grad, lax.optimization_barrier(jnp.sum(proj_all, axis=0)) * scale, lax.optimization_barrier(jnp.sum(gate_all, axis=0)) * scale, lax.optimization_barrier(jnp.sum(out_all, axis=0)) * scale, lax.optimization_barrier(jnp.sum(in_all, axis=0)) * scale, lax.optimization_barrier(jnp.sum(outn_all, axis=0)) * scale)
```

```python
import functools

import jax
import jax.numpy as jnp
from jax import lax
from jax.experimental import pallas as pl
from jax.experimental.pallas import tpu as pltpu
from jax.sharding import PartitionSpec as P

epsilon = 1e-05
f32 = jnp.float32
bf16 = jnp.bfloat16
STEP = 4


def mm(a, b):
    return jnp.dot(a, b, preferred_element_type=f32)


def mm_t(a, b):
    return lax.dot_general(a, b, (((1,), (1,)), ((), ())), preferred_element_type=f32)


def sigmoid(v):
    return 0.5 * jnp.tanh(0.5 * v) + 0.5


def norm_cols(values):
    count = values.shape[0]
    centred = values - jnp.sum(values, axis=0, keepdims=True) * (1.0 / count)
    var = jnp.sum(centred * centred, axis=0, keepdims=True) * (1.0 / count)
    inv_std = lax.rsqrt(var + epsilon)
    return centred * inv_std, inv_std


def norm_back(grad_hat, x_hat, inv_std):
    count = grad_hat.shape[0]
    first = jnp.sum(grad_hat, axis=0, keepdims=True) * (1.0 / count)
    second = jnp.sum(grad_hat * x_hat, axis=0, keepdims=True) * (1.0 / count)
    return (grad_hat - first - x_hat * second) * inv_std


def fold(values, width):
    total = values[:, 0:width]
    for at in range(width, values.shape[1], width):
        total = total + values[:, at : at + width]
    return total


def kernel(
    groups,
    act,
    cot,
    in_gain,
    in_bias,
    w,
    w_t,
    wg,
    wg_t,
    out_gain,
    out_bias,
    wo,
    wo_t,
    eye,
    update,
    pair_grad,
    grads,
    act_all,
    cot_cols,
    left,
    right,
    tri_r,
    tri_c,
    col_act,
    col_cot,
    d_gate_sc,
    sums,
    recv_sem,
    right_sem,
    left_sem,
    cot_send,
    cot_recv,
):
    me = lax.axis_index("dap")
    rows, length, channels = act.shape
    hidden = wo.shape[0]

    barrier = pltpu.get_barrier_semaphore()
    for d in range(1, groups):
        pl.semaphore_signal(
            barrier,
            inc=1,
            device_id={"dap": lax.rem(me + d, groups)},
            device_id_type=pl.DeviceIdType.MESH,
        )
    pl.semaphore_wait(barrier, groups - 1)

    def hop(src, block, send_sems, to):
        return pltpu.make_async_remote_copy(
            src_ref=src,
            dst_ref=act_all.at[block],
            send_sem=send_sems.at[block],
            recv_sem=recv_sem.at[block],
            device_id={"dap": to},
            device_id_type=pl.DeviceIdType.MESH,
        )

    def cot_copy(d):
        peer = lax.rem(me + d, groups)
        at = pl.multiple_of(peer * rows, rows)
        mine = pl.multiple_of(me * rows, rows)
        return pltpu.make_async_remote_copy(
            src_ref=cot.at[:, pl.ds(at, rows), :],
            dst_ref=cot_cols.at[pl.ds(mine, rows)],
            send_sem=cot_send.at[d - 1],
            recv_sem=cot_recv.at[d - 1],
            device_id={"dap": peer},
            device_id_type=pl.DeviceIdType.MESH,
        )

    @pl.when(me + 1 < groups)
    def _():
        hop(act, me, right_sem, me + 1).start()

    @pl.when(me >= 1)
    def _():
        hop(act, me, left_sem, me - 1).start()

    for d in range(1, groups):
        cot_copy(d).start()

    def normed_of(x):
        hat, inv = norm_cols(mm_t(eye[...], x))
        return hat, inv, (hat * in_gain[...] + in_bias[...]).astype(bf16)

    def sides(src, base):
        def body(t, carry):
            x = src[pl.ds(t * STEP, STEP)].reshape(STEP * length, channels)
            _, _, normed = normed_of(x)
            pj = mm(w_t[...], normed)
            lv = sigmoid(pj[0:hidden]) * pj[hidden : 2 * hidden]
            rv = sigmoid(pj[2 * hidden : 3 * hidden]) * pj[3 * hidden : 4 * hidden]
            for r in range(STEP):
                row = base + t * STEP + r
                lanes = slice(r * length, (r + 1) * length)
                left[pl.ds(row, hidden, stride=length), :] = lv[:, lanes]
                right[pl.ds(row, hidden, stride=length), :] = rv[:, lanes]
                own = src[t * STEP + r, pl.ds(pl.multiple_of(me * rows, rows), rows), :]
                col_act[pl.ds(pl.multiple_of(row * rows, rows), rows), :] = own.astype(f32)
            return carry

        lax.fori_loop(0, rows // STEP, body, 0)

    sides(act, me * rows)
    for s in range(1, groups):
        low, high = me - s, me + s

        @pl.when(low >= 0)
        def _():
            hop(act, low, right_sem, me).wait_recv()

            @pl.when(me + 1 < groups)
            def _():
                hop(act_all.at[low], low, right_sem, me + 1).start()

        @pl.when(high < groups)
        def _():
            hop(act, high, left_sem, me).wait_recv()

            @pl.when(me >= 1)
            def _():
                hop(act_all.at[high], high, left_sem, me - 1).start()

        @pl.when(low >= 0)
        def _():
            sides(act_all.at[low], low * rows)

        @pl.when(high < groups)
        def _():
            sides(act_all.at[high], high * rows)

    mine = pl.multiple_of(me * rows, rows)

    def products(h, carry):
        at = pl.multiple_of(h * length, length)
        l_all = left[pl.ds(at, length), :].astype(bf16)
        r_all = right[pl.ds(at, length), :].astype(bf16)
        l_own = left[pl.ds(pl.multiple_of(at + mine, rows), rows), :].astype(bf16)
        r_own = right[pl.ds(pl.multiple_of(at + mine, rows), rows), :].astype(bf16)
        to = pl.ds(pl.multiple_of(h * rows, rows), rows)
        tri_r[to, :] = mm_t(l_own, r_all)
        tri_c[to, :] = mm_t(r_own, l_all)
        return carry

    lax.fori_loop(0, hidden, products, 0, unroll=4)

    def slabs(ref, first):
        return jnp.concatenate(
            [ref[pl.ds(first + r, hidden, stride=rows), :] for r in range(STEP)], axis=1
        )

    def put_slabs(ref, first, values):
        for r in range(STEP):
            ref[pl.ds(first + r, hidden, stride=rows), :] = values[
                :, r * length : (r + 1) * length
            ]

    sums[...] = jnp.zeros_like(sums)
    grads[...] = jnp.zeros_like(grads)
    pw = 4 * hidden

    def row_pass(t, carry):
        first = t * STEP
        x = act[pl.ds(first, STEP)].reshape(STEP * length, channels)
        _, _, normed = normed_of(x)
        gate = sigmoid(mm(wg_t[...], normed))
        hat, inv = norm_cols(slabs(tri_r, first).astype(bf16).astype(f32))
        tri_norm = (hat * out_gain[...] + out_bias[...]).astype(bf16)
        mixed = mm(wo_t[...], tri_norm)
        upd = (gate * mixed).astype(bf16)
        for r in range(STEP):
            update[first + r] = mm_t(eye[...], upd[:, r * length : (r + 1) * length]).astype(bf16)
        cot_t = mm_t(eye[...], cot[pl.ds(first, STEP)].reshape(STEP * length, channels))
        d_mixed_f = cot_t * gate
        d_mixed = d_mixed_f.astype(bf16)
        d_gate = (d_mixed_f * mixed * (1.0 - gate)).astype(bf16)
        d_gate_sc[t] = d_gate
        grads[:, pw : pw + channels] += mm_t(normed, d_gate)
        grads[:, pw + channels : pw + 2 * channels] += mm_t(tri_norm, d_mixed)
        d_out = mm(wo[...], d_mixed)
        sums[2] += fold(d_out * hat, length)
        sums[3] += fold(d_out, length)
        put_slabs(tri_r, first, norm_back(d_out * out_gain[...], hat, inv))
        return carry

    lax.fori_loop(0, rows // STEP, row_pass, 0)

    for d in range(1, groups):
        cot_copy(d).wait_recv()

    def unpack(t, carry):
        to = pl.ds(pl.multiple_of(t * rows, rows), rows)
        col_cot[to, :] = cot_cols[t].astype(f32)
        return carry

    def unpack_own(t, carry):
        to = pl.ds(pl.multiple_of((mine + t) * rows, rows), rows)
        col_cot[to, :] = cot[t, pl.ds(mine, rows), :].astype(f32)
        return carry

    for d in range(1, groups):
        peer = lax.rem(me + d, groups)
        lax.fori_loop(peer * rows, peer * rows + rows, unpack, 0)
    lax.fori_loop(0, rows, unpack_own, 0)

    def columns_of(ref, first):
        return jnp.concatenate(
            [ref[pl.ds(first + r, length, stride=rows), :] for r in range(STEP)], axis=0
        ).astype(bf16)

    def col_pass(t, carry):
        first = t * STEP
        _, _, normed = normed_of(columns_of(col_act, first))
        gate = sigmoid(mm(wg_t[...], normed))
        hat, inv = norm_cols(slabs(tri_c, first).astype(bf16).astype(f32))
        cot_t = mm_t(eye[...], columns_of(col_cot, first))
        d_out = mm(wo[...], (cot_t * gate).astype(bf16))
        put_slabs(tri_c, first, norm_back(d_out * out_gain[...], hat, inv))
        return carry

    lax.fori_loop(0, rows // STEP, col_pass, 0)

    def back_products(h, carry):
        at = pl.multiple_of(h * length, length)
        l_all = left[pl.ds(at, length), :].astype(bf16)
        r_all = right[pl.ds(at, length), :].astype(bf16)
        to = pl.ds(pl.multiple_of(h * rows, rows), rows)
        tri_r[to, :] = mm(tri_r[to, :].astype(bf16), r_all)
        tri_c[to, :] = mm(tri_c[to, :].astype(bf16), l_all)
        return carry

    lax.fori_loop(0, hidden, back_products, 0, unroll=4)

    def last_pass(t, carry):
        first = t * STEP
        x = act[pl.ds(first, STEP)].reshape(STEP * length, channels)
        hat, inv, normed = normed_of(x)
        pj = mm(w_t[...], normed)
        parts = []
        for side, ref in ((0, tri_r), (1, tri_c)):
            grad = slabs(ref, first).astype(bf16).astype(f32)
            sg = sigmoid(pj[2 * side * hidden : (2 * side + 1) * hidden])
            val = pj[(2 * side + 1) * hidden : (2 * side + 2) * hidden]
            d_val = grad * sg
            parts.append((d_val * val * (1.0 - sg)).astype(bf16))
            parts.append(d_val.astype(bf16))
        d_proj = jnp.concatenate(parts, axis=0)
        grads[:, 0:pw] += mm_t(normed, d_proj)
        d_normed = mm(w[...], d_proj) + mm(wg[...], d_gate_sc[t])
        sums[0] += fold(d_normed * hat, length)
        sums[1] += fold(d_normed, length)
        back = norm_back(d_normed * in_gain[...], hat, inv).astype(bf16)
        for r in range(STEP):
            pair_grad[first + r] = mm_t(eye[...], back[:, r * length : (r + 1) * length]).astype(
                bf16
            )
        return carry

    lax.fori_loop(0, rows // STEP, last_pass, 0)

    for n in range(4):
        at = pw + 2 * channels + n * 8
        grads[:, at : at + 8] = jnp.broadcast_to(
            jnp.sum(sums[n], axis=1, keepdims=True), (channels, 8)
        )

    for s in range(groups):
        low, high = me - s, me + s

        @pl.when((low >= 0) & (me + 1 < groups))
        def _():
            hop(act, low, right_sem, me + 1).wait_send()

        @pl.when((high < groups) & (me >= 1))
        def _():
            hop(act, high, left_sem, me - 1).wait_send()

    for d in range(1, groups):
        cot_copy(d).wait_send()


def shards(
    groups,
    pair_act,
    pair_cot,
    in_gain,
    in_bias,
    proj_weight,
    gate_weight,
    out_gain,
    out_bias,
    out_weight,
):
    _, rows, length, channels = pair_act.shape
    hidden = out_weight.shape[0]
    act = pair_act.reshape(rows, length, channels)
    cot = pair_cot.reshape(rows, length, channels)
    width = 4 * hidden + 3 * channels
    vmem = pl.BlockSpec(memory_space=pltpu.VMEM)
    dma = pltpu.SemaphoreType.DMA
    update, pair_grad, grads = pl.pallas_call(
        functools.partial(kernel, groups),
        out_shape=(
            jax.ShapeDtypeStruct(act.shape, bf16),
            jax.ShapeDtypeStruct(act.shape, bf16),
            jax.ShapeDtypeStruct((channels, width), f32),
        ),
        in_specs=[vmem] * 13,
        out_specs=(vmem,) * 3,
        scratch_shapes=[
            pltpu.VMEM((groups, rows, length, channels), bf16),
            pltpu.VMEM((length, rows, channels), bf16),
            pltpu.VMEM((hidden * length, length), f32),
            pltpu.VMEM((hidden * length, length), f32),
            pltpu.VMEM((hidden * rows, length), f32),
            pltpu.VMEM((hidden * rows, length), f32),
            pltpu.VMEM((length * rows, channels), f32),
            pltpu.VMEM((length * rows, channels), f32),
            pltpu.VMEM((rows // STEP, channels, STEP * length), bf16),
            pltpu.VMEM((4, channels, length), f32),
            dma((groups,)),
            dma((groups,)),
            dma((groups,)),
            dma((groups - 1,)),
            dma((groups - 1,)),
        ],
        compiler_params=pltpu.CompilerParams(
            collective_id=0, has_side_effects=True, vmem_limit_bytes=60 * 1024 * 1024
        ),
        name="tri",
    )(
        act,
        cot,
        in_gain.reshape(channels, 1),
        in_bias.reshape(channels, 1),
        proj_weight,
        proj_weight.T,
        gate_weight,
        gate_weight.T,
        out_gain.reshape(hidden, 1),
        out_bias.reshape(hidden, 1),
        out_weight,
        out_weight.T,
        jnp.eye(channels, dtype=bf16),
    )
    total = lax.psum(grads, ("dp", "dap")) * (1.0 / length)
    a = 4 * hidden
    b = a + channels
    c = b + channels
    stats = total[:, c : c + 32 : 8].T
    return (
        update.reshape(pair_act.shape),
        pair_grad.reshape(pair_act.shape),
        total[:, 0:a],
        total[:, a:b],
        total[:, b:c],
        stats[0:2],
        stats[2:4],
    )


def solution(mesh):
    placed = (P("dp", "dap", None, None),) * 2 + (P(),) * 7
    return jax.shard_map(
        functools.partial(shards, mesh.shape["dap"]),
        mesh=mesh,
        in_specs=placed,
        out_specs=(P("dp", "dap", None, None), P("dp", "dap", None, None), P(), P(), P(), P(), P()),
        check_vma=False,
    )
```

```python
import functools

import jax
import jax.numpy as jnp
from jax import lax
from jax.experimental import pallas as pl
from jax.experimental.pallas import tpu as pltpu
from jax.sharding import PartitionSpec as P

epsilon = 1e-05
f32 = jnp.float32
bf16 = jnp.bfloat16
STEP = 4


def mm(a, b):
    return jnp.dot(a, b, preferred_element_type=f32)


def mm_t(a, b):
    return lax.dot_general(a, b, (((1,), (1,)), ((), ())), preferred_element_type=f32)


def sigmoid(v):
    return 0.5 * jnp.tanh(0.5 * v) + 0.5


def norm_cols(values):
    count = values.shape[0]
    centred = values - jnp.sum(values, axis=0, keepdims=True) * (1.0 / count)
    var = jnp.sum(centred * centred, axis=0, keepdims=True) * (1.0 / count)
    inv_std = lax.rsqrt(var + epsilon)
    return centred * inv_std, inv_std


def norm_back(grad_hat, x_hat, inv_std):
    count = grad_hat.shape[0]
    first = jnp.sum(grad_hat, axis=0, keepdims=True) * (1.0 / count)
    second = jnp.sum(grad_hat * x_hat, axis=0, keepdims=True) * (1.0 / count)
    return (grad_hat - first - x_hat * second) * inv_std


def fold(values, width):
    total = values[:, 0:width]
    for at in range(width, values.shape[1], width):
        total = total + values[:, at : at + width]
    return total


def kernel(
    crops,
    groups,
    act,
    cot,
    in_gain_row,
    in_bias_row,
    w,
    wg,
    out_gain_row,
    out_bias_row,
    wo,
    update,
    pair_grad,
    proj_grad,
    gate_grad,
    out_grad,
    in_norm_grad,
    out_norm_grad,
    act_all,
    cot_cols,
    left,
    right,
    tri_r,
    tri_c,
    col_act,
    col_cot,
    d_gate_sc,
    sums,
    recv_sem,
    right_sem,
    left_sem,
    cot_send,
    cot_recv,
    w_t,
    wg_t,
    wo_t,
    eye,
    columns,
    early,
    late,
    early_bufs,
    late_bufs,
    sum_sems,
    swap_sems,
):
    me = lax.axis_index("dap")
    crop = lax.axis_index("dp")
    rows, length, channels = act.shape
    hidden = wo.shape[0]

    barrier = pltpu.get_barrier_semaphore()
    for d in range(1, groups):
        pl.semaphore_signal(
            barrier,
            inc=1,
            device_id={"dap": lax.rem(me + d, groups)},
            device_id_type=pl.DeviceIdType.MESH,
        )
    for d in range(1, crops):
        pl.semaphore_signal(
            barrier,
            inc=1,
            device_id={"dp": lax.rem(crop + d, crops)},
            device_id_type=pl.DeviceIdType.MESH,
        )
    pl.semaphore_wait(barrier, groups + crops - 2)

    def hop(src, block, send_sems, to):
        return pltpu.make_async_remote_copy(
            src_ref=src,
            dst_ref=act_all.at[block],
            send_sem=send_sems.at[block],
            recv_sem=recv_sem.at[block],
            device_id={"dap": to},
            device_id_type=pl.DeviceIdType.MESH,
        )

    def cot_copy(d):
        peer = lax.rem(me + d, groups)
        at = pl.multiple_of(peer * rows, rows)
        mine = pl.multiple_of(me * rows, rows)
        return pltpu.make_async_remote_copy(
            src_ref=cot.at[:, pl.ds(at, rows), :],
            dst_ref=cot_cols.at[pl.ds(mine, rows)],
            send_sem=cot_send.at[d - 1],
            recv_sem=cot_recv.at[d - 1],
            device_id={"dap": peer},
            device_id_type=pl.DeviceIdType.MESH,
        )

    @pl.when(me + 1 < groups)
    def _():
        hop(act, me, right_sem, me + 1).start()

    @pl.when(me >= 1)
    def _():
        hop(act, me, left_sem, me - 1).start()

    for d in range(1, groups):
        cot_copy(d).start()

    def turned(block):
        return jnp.transpose(block.astype(f32)).astype(bf16)

    for n in range(4):
        w_t[n * hidden : (n + 1) * hidden, :] = turned(w[:, n * hidden : (n + 1) * hidden])
    wg_t[...] = turned(wg[...])
    wo_t[...] = turned(wo[...])
    square = (channels, channels)
    eye[...] = (
        (lax.broadcasted_iota(jnp.int32, square, 0) == lax.broadcasted_iota(jnp.int32, square, 1))
        .astype(f32)
        .astype(bf16)
    )
    for n, row in enumerate((in_gain_row, in_bias_row, out_gain_row, out_bias_row)):
        columns[n] = jnp.transpose(jnp.broadcast_to(row[...], square))[:, 0:1]
    in_gain, in_bias, out_gain, out_bias = (columns.at[n] for n in range(4))

    def piece_copy(which, stage, bufs, e):
        peer = lax.rem(crop + e, crops)
        sent, got, _, total = bufs
        src, dst = (sent.at[peer], got.at[crop]) if stage == 0 else (total.at[crop],) * 2
        return pltpu.make_async_remote_copy(
            src_ref=src,
            dst_ref=dst,
            send_sem=sum_sems.at[which, stage, 0, e - 1],
            recv_sem=sum_sems.at[which, stage, 1, e - 1],
            device_id={"dp": peer},
            device_id_type=pl.DeviceIdType.MESH,
        )

    def swap_copy(which, bufs, d):
        part = bufs[2]
        return pltpu.make_async_remote_copy(
            src_ref=part.at[me],
            dst_ref=part.at[me],
            send_sem=swap_sems.at[which, 0, d - 1],
            recv_sem=swap_sems.at[which, 1, d - 1],
            device_id={"dap": lax.rem(me + d, groups)},
            device_id_type=pl.DeviceIdType.MESH,
        )

    piece = channels // crops

    def sum_first(which, acc, bufs):
        for p in range(crops):
            bufs[0][p] = acc[p * piece : (p + 1) * piece, :]
        for e in range(1, crops):
            piece_copy(which, 0, bufs, e).start()

    def sum_second(which, bufs):
        total = bufs[0][crop]
        for e in range(1, crops):
            piece_copy(which, 0, bufs, e).wait_recv()
            total = total + bufs[1][lax.rem(crop + crops - e, crops)]
        bufs[2][me] = total
        for d in range(1, groups):
            swap_copy(which, bufs, d).start()

    def sum_third(which, bufs):
        for d in range(1, groups):
            swap_copy(which, bufs, d).wait_recv()
        total = bufs[2][0]
        for g in range(1, groups):
            total = total + bufs[2][g]
        bufs[3][crop] = total * (1.0 / length)
        for e in range(1, crops):
            piece_copy(which, 1, bufs, e).start()

    def sum_last(which, bufs, outs, stats_out):
        for e in range(1, crops):
            piece_copy(which, 1, bufs, e).wait_recv()
        total = jnp.concatenate([bufs[3][p] for p in range(crops)], axis=0)
        at = 0
        for out in outs:
            out[...] = total[:, at : at + out.shape[1]]
            at += out.shape[1]
        turned_stats = jnp.transpose(total[:, at : at + channels])
        stats_out[0:1, :] = turned_stats[0:1]
        stats_out[1:2, :] = turned_stats[8:9]
        for e in range(1, crops):
            piece_copy(which, 0, bufs, e).wait_send()
            piece_copy(which, 1, bufs, e).wait_send()
        for d in range(1, groups):
            swap_copy(which, bufs, d).wait_send()

    def put_stats(acc, first):
        at = acc.shape[1] - channels
        for n in range(2):
            acc[:, at + 8 * n : at + 8 * n + 8] = jnp.broadcast_to(
                jnp.sum(sums[first + n], axis=1, keepdims=True), (channels, 8)
            )

    def normed_of(x):
        hat, inv = norm_cols(mm_t(eye[...], x))
        return hat, inv, (hat * in_gain[...] + in_bias[...]).astype(bf16)

    def sides(src, base):
        def body(t, carry):
            x = src[pl.ds(t * STEP, STEP)].reshape(STEP * length, channels)
            _, _, normed = normed_of(x)
            pj = mm(w_t[...], normed)
            lv = sigmoid(pj[0:hidden]) * pj[hidden : 2 * hidden]
            rv = sigmoid(pj[2 * hidden : 3 * hidden]) * pj[3 * hidden : 4 * hidden]
            for r in range(STEP):
                row = base + t * STEP + r
                lanes = slice(r * length, (r + 1) * length)
                left[pl.ds(row, hidden, stride=length), :] = lv[:, lanes]
                right[pl.ds(row, hidden, stride=length), :] = rv[:, lanes]
                own = src[t * STEP + r, pl.ds(pl.multiple_of(me * rows, rows), rows), :]
                col_act[pl.ds(pl.multiple_of(row * rows, rows), rows), :] = own.astype(f32)
            return carry

        lax.fori_loop(0, rows // STEP, body, 0)

    sides(act, me * rows)
    for s in range(1, groups):
        low, high = me - s, me + s

        @pl.when(low >= 0)
        def _():
            hop(act, low, right_sem, me).wait_recv()

            @pl.when(me + 1 < groups)
            def _():
                hop(act_all.at[low], low, right_sem, me + 1).start()

        @pl.when(high < groups)
        def _():
            hop(act, high, left_sem, me).wait_recv()

            @pl.when(me >= 1)
            def _():
                hop(act_all.at[high], high, left_sem, me - 1).start()

        @pl.when(low >= 0)
        def _():
            sides(act_all.at[low], low * rows)

        @pl.when(high < groups)
        def _():
            sides(act_all.at[high], high * rows)

    mine = pl.multiple_of(me * rows, rows)

    def products(h, carry):
        at = pl.multiple_of(h * length, length)
        l_all = left[pl.ds(at, length), :].astype(bf16)
        r_all = right[pl.ds(at, length), :].astype(bf16)
        l_own = left[pl.ds(pl.multiple_of(at + mine, rows), rows), :].astype(bf16)
        r_own = right[pl.ds(pl.multiple_of(at + mine, rows), rows), :].astype(bf16)
        to = pl.ds(pl.multiple_of(h * rows, rows), rows)
        tri_r[to, :] = mm_t(l_own, r_all)
        tri_c[to, :] = mm_t(r_own, l_all)
        return carry

    lax.fori_loop(0, hidden, products, 0, unroll=4)

    def slabs(ref, first):
        return jnp.concatenate(
            [ref[pl.ds(first + r, hidden, stride=rows), :] for r in range(STEP)], axis=1
        )

    def put_slabs(ref, first, values):
        for r in range(STEP):
            ref[pl.ds(first + r, hidden, stride=rows), :] = values[
                :, r * length : (r + 1) * length
            ]

    sums[...] = jnp.zeros_like(sums)
    early[...] = jnp.zeros_like(early)
    late[...] = jnp.zeros_like(late)
    pw = 4 * hidden

    def row_pass(t, carry):
        first = t * STEP
        x = act[pl.ds(first, STEP)].reshape(STEP * length, channels)
        _, _, normed = normed_of(x)
        gate = sigmoid(mm(wg_t[...], normed))
        hat, inv = norm_cols(slabs(tri_r, first).astype(bf16).astype(f32))
        tri_norm = (hat * out_gain[...] + out_bias[...]).astype(bf16)
        mixed = mm(wo_t[...], tri_norm)
        upd = (gate * mixed).astype(bf16)
        for r in range(STEP):
            update[first + r] = mm_t(eye[...], upd[:, r * length : (r + 1) * length]).astype(bf16)
        cot_t = mm_t(eye[...], cot[pl.ds(first, STEP)].reshape(STEP * length, channels))
        d_mixed_f = cot_t * gate
        d_mixed = d_mixed_f.astype(bf16)
        d_gate = (d_mixed_f * mixed * (1.0 - gate)).astype(bf16)
        d_gate_sc[t] = d_gate
        early[:, 0:channels] += mm_t(normed, d_gate)
        early[:, channels : 2 * channels] += mm_t(tri_norm, d_mixed)
        d_out = mm(wo[...], d_mixed)
        sums[2] += fold(d_out * hat, length)
        sums[3] += fold(d_out, length)
        put_slabs(tri_r, first, norm_back(d_out * out_gain[...], hat, inv))
        return carry

    lax.fori_loop(0, rows // STEP, row_pass, 0)
    put_stats(early, 2)
    sum_first(0, early, early_bufs)

    for d in range(1, groups):
        cot_copy(d).wait_recv()

    def unpack(t, carry):
        to = pl.ds(pl.multiple_of(t * rows, rows), rows)
        col_cot[to, :] = cot_cols[t].astype(f32)
        return carry

    def unpack_own(t, carry):
        to = pl.ds(pl.multiple_of((mine + t) * rows, rows), rows)
        col_cot[to, :] = cot[t, pl.ds(mine, rows), :].astype(f32)
        return carry

    for d in range(1, groups):
        peer = lax.rem(me + d, groups)
        lax.fori_loop(peer * rows, peer * rows + rows, unpack, 0)
    lax.fori_loop(0, rows, unpack_own, 0)

    def columns_of(ref, first):
        return jnp.concatenate(
            [ref[pl.ds(first + r, length, stride=rows), :] for r in range(STEP)], axis=0
        ).astype(bf16)

    def col_pass(t, carry):
        first = t * STEP
        _, _, normed = normed_of(columns_of(col_act, first))
        gate = sigmoid(mm(wg_t[...], normed))
        hat, inv = norm_cols(slabs(tri_c, first).astype(bf16).astype(f32))
        cot_t = mm_t(eye[...], columns_of(col_cot, first))
        d_out = mm(wo[...], (cot_t * gate).astype(bf16))
        put_slabs(tri_c, first, norm_back(d_out * out_gain[...], hat, inv))
        return carry

    lax.fori_loop(0, rows // STEP, col_pass, 0)
    sum_second(0, early_bufs)

    def back_products(h, carry):
        at = pl.multiple_of(h * length, length)
        l_all = left[pl.ds(at, length), :].astype(bf16)
        r_all = right[pl.ds(at, length), :].astype(bf16)
        to = pl.ds(pl.multiple_of(h * rows, rows), rows)
        tri_r[to, :] = mm(tri_r[to, :].astype(bf16), r_all)
        tri_c[to, :] = mm(tri_c[to, :].astype(bf16), l_all)
        return carry

    lax.fori_loop(0, hidden, back_products, 0, unroll=4)
    sum_third(0, early_bufs)

    def last_pass(t, carry):
        first = t * STEP
        x = act[pl.ds(first, STEP)].reshape(STEP * length, channels)
        hat, inv, normed = normed_of(x)
        pj = mm(w_t[...], normed)
        parts = []
        for side, ref in ((0, tri_r), (1, tri_c)):
            grad = slabs(ref, first).astype(bf16).astype(f32)
            sg = sigmoid(pj[2 * side * hidden : (2 * side + 1) * hidden])
            val = pj[(2 * side + 1) * hidden : (2 * side + 2) * hidden]
            d_val = grad * sg
            parts.append((d_val * val * (1.0 - sg)).astype(bf16))
            parts.append(d_val.astype(bf16))
        d_proj = jnp.concatenate(parts, axis=0)
        late[:, 0:pw] += mm_t(normed, d_proj)
        d_normed = mm(w[...], d_proj) + mm(wg[...], d_gate_sc[t])
        sums[0] += fold(d_normed * hat, length)
        sums[1] += fold(d_normed, length)
        back = norm_back(d_normed * in_gain[...], hat, inv).astype(bf16)
        for r in range(STEP):
            pair_grad[first + r] = mm_t(eye[...], back[:, r * length : (r + 1) * length]).astype(
                bf16
            )
        return carry

    lax.fori_loop(0, rows // STEP, last_pass, 0)

    put_stats(late, 0)
    sum_first(1, late, late_bufs)
    sum_last(0, early_bufs, (gate_grad, out_grad), out_norm_grad)
    sum_second(1, late_bufs)
    sum_third(1, late_bufs)
    sum_last(1, late_bufs, (proj_grad,), in_norm_grad)

    for s in range(groups):
        low, high = me - s, me + s

        @pl.when((low >= 0) & (me + 1 < groups))
        def _():
            hop(act, low, right_sem, me + 1).wait_send()

        @pl.when((high < groups) & (me >= 1))
        def _():
            hop(act, high, left_sem, me - 1).wait_send()

    for d in range(1, groups):
        cot_copy(d).wait_send()


def shards(
    crops,
    groups,
    pair_act,
    pair_cot,
    in_gain,
    in_bias,
    proj_weight,
    gate_weight,
    out_gain,
    out_bias,
    out_weight,
):
    _, rows, length, channels = pair_act.shape
    hidden = out_weight.shape[0]
    act = pair_act.reshape(rows, length, channels)
    cot = pair_cot.reshape(rows, length, channels)
    vmem = pl.BlockSpec(memory_space=pltpu.VMEM)
    dma = pltpu.SemaphoreType.DMA
    piece = channels // crops

    def sum_bufs(width):
        return tuple(pltpu.VMEM((n, piece, width), f32) for n in (crops, crops, groups, crops))

    early_width, late_width = 3 * channels, 4 * hidden + channels
    update, pair_grad, *grads = pl.pallas_call(
        functools.partial(kernel, crops, groups),
        out_shape=(
            jax.ShapeDtypeStruct(act.shape, bf16),
            jax.ShapeDtypeStruct(act.shape, bf16),
            jax.ShapeDtypeStruct(proj_weight.shape, f32),
            jax.ShapeDtypeStruct(gate_weight.shape, f32),
            jax.ShapeDtypeStruct(out_weight.shape, f32),
            jax.ShapeDtypeStruct((2, channels), f32),
            jax.ShapeDtypeStruct((2, hidden), f32),
        ),
        in_specs=[vmem] * 9,
        out_specs=(vmem,) * 7,
        scratch_shapes=[
            pltpu.VMEM((groups, rows, length, channels), bf16),
            pltpu.VMEM((length, rows, channels), bf16),
            pltpu.VMEM((hidden * length, length), f32),
            pltpu.VMEM((hidden * length, length), f32),
            pltpu.VMEM((hidden * rows, length), f32),
            pltpu.VMEM((hidden * rows, length), f32),
            pltpu.VMEM((length * rows, channels), f32),
            pltpu.VMEM((length * rows, channels), f32),
            pltpu.VMEM((rows // STEP, channels, STEP * length), bf16),
            pltpu.VMEM((4, channels, length), f32),
            dma((groups,)),
            dma((groups,)),
            dma((groups,)),
            dma((groups - 1,)),
            dma((groups - 1,)),
            pltpu.VMEM((4 * hidden, channels), bf16),
            pltpu.VMEM((channels, channels), bf16),
            pltpu.VMEM((channels, hidden), bf16),
            pltpu.VMEM((channels, channels), bf16),
            pltpu.VMEM((4, channels, 1), f32),
            pltpu.VMEM((channels, early_width), f32),
            pltpu.VMEM((channels, late_width), f32),
            sum_bufs(early_width),
            sum_bufs(late_width),
            dma((2, 2, 2, crops - 1)),
            dma((2, 2, groups - 1)),
        ],
        compiler_params=pltpu.CompilerParams(
            collective_id=0, has_side_effects=True, vmem_limit_bytes=60 * 1024 * 1024
        ),
        name="tri",
    )(
        act,
        cot,
        in_gain.reshape(1, channels),
        in_bias.reshape(1, channels),
        proj_weight,
        gate_weight,
        out_gain.reshape(1, hidden),
        out_bias.reshape(1, hidden),
        out_weight,
    )
    return (update.reshape(pair_act.shape), pair_grad.reshape(pair_act.shape), *grads)


def solution(mesh):
    placed = (P("dp", "dap", None, None),) * 2 + (P(),) * 7
    return jax.shard_map(
        functools.partial(shards, mesh.shape["dp"], mesh.shape["dap"]),
        mesh=mesh,
        in_specs=placed,
        out_specs=(P("dp", "dap", None, None), P("dp", "dap", None, None), P(), P(), P(), P(), P()),
        check_vma=False,
    )
```

```python
import functools

import jax
import jax.numpy as jnp
from jax import lax
from jax.experimental import pallas as pl
from jax.experimental.pallas import tpu as pltpu
from jax.sharding import PartitionSpec as P

epsilon = 1e-05
f32 = jnp.float32
bf16 = jnp.bfloat16
STEP = 4


def mm(a, b):
    return jnp.dot(a, b, preferred_element_type=f32)


def mm_t(a, b):
    return lax.dot_general(a, b, (((1,), (1,)), ((), ())), preferred_element_type=f32)


def sigmoid(v):
    return 0.5 * jnp.tanh(0.5 * v) + 0.5


def norm_cols(values):
    count = values.shape[0]
    centred = values - jnp.sum(values, axis=0, keepdims=True) * (1.0 / count)
    var = jnp.sum(centred * centred, axis=0, keepdims=True) * (1.0 / count)
    inv_std = lax.rsqrt(var + epsilon)
    return centred * inv_std, inv_std


def norm_back(grad_hat, x_hat, inv_std):
    count = grad_hat.shape[0]
    first = jnp.sum(grad_hat, axis=0, keepdims=True) * (1.0 / count)
    second = jnp.sum(grad_hat * x_hat, axis=0, keepdims=True) * (1.0 / count)
    return (grad_hat - first - x_hat * second) * inv_std


def fold(values, width):
    total = values[:, 0:width]
    for at in range(width, values.shape[1], width):
        total = total + values[:, at : at + width]
    return total


def kernel(
    crops,
    groups,
    act,
    cot,
    in_gain_row,
    in_bias_row,
    w,
    wg,
    out_gain_row,
    out_bias_row,
    wo,
    update,
    pair_grad,
    proj_grad,
    gate_grad,
    out_grad,
    in_norm_grad,
    out_norm_grad,
    act_all,
    cot_cols,
    left,
    right,
    tri_r,
    tri_c,
    col_act,
    col_cot,
    d_gate_sc,
    sums,
    recv_sem,
    right_sem,
    left_sem,
    cot_send,
    cot_recv,
    w_t,
    wg_t,
    wo_t,
    eye,
    columns,
    early,
    late,
    early_bufs,
    late_bufs,
    sum_sems,
    swap_sems,
    d_normed_sc,
):
    me = lax.axis_index("dap")
    crop = lax.axis_index("dp")
    rows, length, channels = act.shape
    hidden = wo.shape[0]

    barrier = pltpu.get_barrier_semaphore()
    for d in range(1, groups):
        pl.semaphore_signal(
            barrier,
            inc=1,
            device_id={"dap": lax.rem(me + d, groups)},
            device_id_type=pl.DeviceIdType.MESH,
        )
    for d in range(1, crops):
        pl.semaphore_signal(
            barrier,
            inc=1,
            device_id={"dp": lax.rem(crop + d, crops)},
            device_id_type=pl.DeviceIdType.MESH,
        )
    pl.semaphore_wait(barrier, groups + crops - 2)

    def hop(src, block, send_sems, to):
        return pltpu.make_async_remote_copy(
            src_ref=src,
            dst_ref=act_all.at[block],
            send_sem=send_sems.at[block],
            recv_sem=recv_sem.at[block],
            device_id={"dap": to},
            device_id_type=pl.DeviceIdType.MESH,
        )

    def cot_copy(d):
        peer = lax.rem(me + d, groups)
        at = pl.multiple_of(peer * rows, rows)
        mine = pl.multiple_of(me * rows, rows)
        return pltpu.make_async_remote_copy(
            src_ref=cot.at[:, pl.ds(at, rows), :],
            dst_ref=cot_cols.at[pl.ds(mine, rows)],
            send_sem=cot_send.at[d - 1],
            recv_sem=cot_recv.at[d - 1],
            device_id={"dap": peer},
            device_id_type=pl.DeviceIdType.MESH,
        )

    @pl.when(me + 1 < groups)
    def _():
        hop(act, me, right_sem, me + 1).start()

    @pl.when(me >= 1)
    def _():
        hop(act, me, left_sem, me - 1).start()

    def turned(block):
        return jnp.transpose(block.astype(f32)).astype(bf16)

    for n in range(4):
        w_t[n * hidden : (n + 1) * hidden, :] = turned(w[:, n * hidden : (n + 1) * hidden])
    wg_t[...] = turned(wg[...])
    wo_t[...] = turned(wo[...])
    square = (channels, channels)
    eye[...] = (
        (lax.broadcasted_iota(jnp.int32, square, 0) == lax.broadcasted_iota(jnp.int32, square, 1))
        .astype(f32)
        .astype(bf16)
    )
    for n, row in enumerate((in_gain_row, in_bias_row, out_gain_row, out_bias_row)):
        columns[n] = jnp.transpose(jnp.broadcast_to(row[...], square))[:, 0:1]
    in_gain, in_bias, out_gain, out_bias = (columns.at[n] for n in range(4))

    def piece_copy(which, stage, bufs, e):
        peer = lax.rem(crop + e, crops)
        sent, got, _, total = bufs
        src, dst = (sent.at[peer], got.at[crop]) if stage == 0 else (total.at[crop],) * 2
        return pltpu.make_async_remote_copy(
            src_ref=src,
            dst_ref=dst,
            send_sem=sum_sems.at[which, stage, 0, e - 1],
            recv_sem=sum_sems.at[which, stage, 1, e - 1],
            device_id={"dp": peer},
            device_id_type=pl.DeviceIdType.MESH,
        )

    def swap_copy(which, bufs, d):
        part = bufs[2]
        return pltpu.make_async_remote_copy(
            src_ref=part.at[me],
            dst_ref=part.at[me],
            send_sem=swap_sems.at[which, 0, d - 1],
            recv_sem=swap_sems.at[which, 1, d - 1],
            device_id={"dap": lax.rem(me + d, groups)},
            device_id_type=pl.DeviceIdType.MESH,
        )

    piece = channels // crops

    def sum_first(which, acc, bufs):
        for p in range(crops):
            bufs[0][p] = acc[p * piece : (p + 1) * piece, :]
        for e in range(1, crops):
            piece_copy(which, 0, bufs, e).start()

    def sum_second(which, bufs):
        total = bufs[0][crop]
        for e in range(1, crops):
            piece_copy(which, 0, bufs, e).wait_recv()
            total = total + bufs[1][lax.rem(crop + crops - e, crops)]
        bufs[2][me] = total
        for d in range(1, groups):
            swap_copy(which, bufs, d).start()

    def sum_third(which, bufs):
        for d in range(1, groups):
            swap_copy(which, bufs, d).wait_recv()
        total = bufs[2][0]
        for g in range(1, groups):
            total = total + bufs[2][g]
        bufs[3][crop] = total * (1.0 / length)
        for e in range(1, crops):
            piece_copy(which, 1, bufs, e).start()

    def sum_last(which, bufs, outs, stats_out):
        for e in range(1, crops):
            piece_copy(which, 1, bufs, e).wait_recv()
        total = jnp.concatenate([bufs[3][p] for p in range(crops)], axis=0)
        at = 0
        for out in outs:
            out[...] = total[:, at : at + out.shape[1]]
            at += out.shape[1]
        turned_stats = jnp.transpose(total[:, at : at + channels])
        stats_out[0:1, :] = turned_stats[0:1]
        stats_out[1:2, :] = turned_stats[8:9]
        for e in range(1, crops):
            piece_copy(which, 0, bufs, e).wait_send()
            piece_copy(which, 1, bufs, e).wait_send()
        for d in range(1, groups):
            swap_copy(which, bufs, d).wait_send()

    def put_stats(acc, first):
        at = acc.shape[1] - channels
        for n in range(2):
            acc[:, at + 8 * n : at + 8 * n + 8] = jnp.broadcast_to(
                jnp.sum(sums[first + n], axis=1, keepdims=True), (channels, 8)
            )

    def normed_of(x):
        hat, inv = norm_cols(mm_t(eye[...], x))
        return hat, inv, (hat * in_gain[...] + in_bias[...]).astype(bf16)

    def sides(src, base):
        def body(t, carry):
            x = src[pl.ds(t * STEP, STEP)].reshape(STEP * length, channels)
            _, _, normed = normed_of(x)
            pj = mm(w_t[...], normed)
            lv = sigmoid(pj[0:hidden]) * pj[hidden : 2 * hidden]
            rv = sigmoid(pj[2 * hidden : 3 * hidden]) * pj[3 * hidden : 4 * hidden]
            for r in range(STEP):
                row = base + t * STEP + r
                lanes = slice(r * length, (r + 1) * length)
                left[pl.ds(row, hidden, stride=length), :] = lv[:, lanes]
                right[pl.ds(row, hidden, stride=length), :] = rv[:, lanes]
                own = src[t * STEP + r, pl.ds(pl.multiple_of(me * rows, rows), rows), :]
                col_act[pl.ds(pl.multiple_of(row * rows, rows), rows), :] = own.astype(f32)
            return carry

        lax.fori_loop(0, rows // STEP, body, 0)

    sides(act, me * rows)
    for s in range(1, groups):
        low, high = me - s, me + s

        @pl.when(low >= 0)
        def _():
            hop(act, low, right_sem, me).wait_recv()

            @pl.when(me + 1 < groups)
            def _():
                hop(act_all.at[low], low, right_sem, me + 1).start()

        @pl.when(high < groups)
        def _():
            hop(act, high, left_sem, me).wait_recv()

            @pl.when(me >= 1)
            def _():
                hop(act_all.at[high], high, left_sem, me - 1).start()

        if s == groups - 1:
            for d in range(1, groups):
                cot_copy(d).start()

        @pl.when(low >= 0)
        def _():
            sides(act_all.at[low], low * rows)

        @pl.when(high < groups)
        def _():
            sides(act_all.at[high], high * rows)

    mine = pl.multiple_of(me * rows, rows)

    def products(h, carry):
        at = pl.multiple_of(h * length, length)
        l_all = left[pl.ds(at, length), :].astype(bf16)
        r_all = right[pl.ds(at, length), :].astype(bf16)
        l_own = left[pl.ds(pl.multiple_of(at + mine, rows), rows), :].astype(bf16)
        r_own = right[pl.ds(pl.multiple_of(at + mine, rows), rows), :].astype(bf16)
        to = pl.ds(pl.multiple_of(h * rows, rows), rows)
        tri_r[to, :] = mm_t(l_own, r_all)
        tri_c[to, :] = mm_t(r_own, l_all)
        return carry

    lax.fori_loop(0, hidden, products, 0, unroll=4)

    def slabs(ref, first):
        return jnp.concatenate(
            [ref[pl.ds(first + r, hidden, stride=rows), :] for r in range(STEP)], axis=1
        )

    def put_slabs(ref, first, values):
        for r in range(STEP):
            ref[pl.ds(first + r, hidden, stride=rows), :] = values[
                :, r * length : (r + 1) * length
            ]

    sums[...] = jnp.zeros_like(sums)
    early[...] = jnp.zeros_like(early)
    late[...] = jnp.zeros_like(late)

    def row_pass(t, carry):
        first = t * STEP
        x = act[pl.ds(first, STEP)].reshape(STEP * length, channels)
        _, _, normed = normed_of(x)
        gate = sigmoid(mm(wg_t[...], normed))
        hat, inv = norm_cols(slabs(tri_r, first).astype(bf16).astype(f32))
        tri_norm = (hat * out_gain[...] + out_bias[...]).astype(bf16)
        mixed = mm(wo_t[...], tri_norm)
        upd = (gate * mixed).astype(bf16)
        for r in range(STEP):
            update[first + r] = mm_t(eye[...], upd[:, r * length : (r + 1) * length]).astype(bf16)
        cot_t = mm_t(eye[...], cot[pl.ds(first, STEP)].reshape(STEP * length, channels))
        d_mixed_f = cot_t * gate
        d_mixed = d_mixed_f.astype(bf16)
        d_gate = (d_mixed_f * mixed * (1.0 - gate)).astype(bf16)
        d_gate_sc[t] = d_gate
        early[:, 0:channels] += mm_t(normed, d_gate)
        early[:, channels : 2 * channels] += mm_t(tri_norm, d_mixed)
        d_out = mm(wo[...], d_mixed)
        sums[2] += fold(d_out * hat, length)
        sums[3] += fold(d_out, length)
        put_slabs(tri_r, first, norm_back(d_out * out_gain[...], hat, inv))
        return carry

    lax.fori_loop(0, rows // STEP, row_pass, 0)

    def back_rows(h, carry):
        r_all = right[pl.ds(pl.multiple_of(h * length, length), length), :].astype(bf16)
        to = pl.ds(pl.multiple_of(h * rows, rows), rows)
        tri_r[to, :] = mm(tri_r[to, :].astype(bf16), r_all)
        return carry

    lax.fori_loop(0, hidden, back_rows, 0, unroll=8)

    half = 2 * hidden

    def half_grad(ref, first, pj):
        grad = slabs(ref, first).astype(bf16).astype(f32)
        sg = sigmoid(pj[0:hidden])
        d_val = grad * sg
        d_pre = d_val * pj[hidden:half] * (1.0 - sg)
        return jnp.concatenate([d_pre.astype(bf16), d_val.astype(bf16)], axis=0)

    def left_pass(t, carry):
        first = t * STEP
        x = act[pl.ds(first, STEP)].reshape(STEP * length, channels)
        _, _, normed = normed_of(x)
        d_proj = half_grad(tri_r, first, mm(w_t[0:half, :], normed))
        early[:, 2 * channels : 2 * channels + half] += mm_t(normed, d_proj)
        d_normed_sc[t] = mm(w[:, 0:half], d_proj) + mm(wg[...], d_gate_sc[t])
        return carry

    lax.fori_loop(0, rows // STEP, left_pass, 0)
    put_stats(early, 2)
    sum_first(0, early, early_bufs)

    def unpack(t, carry):
        to = pl.ds(pl.multiple_of(t * rows, rows), rows)
        col_cot[to, :] = cot_cols[t].astype(f32)
        return carry

    def unpack_own(t, carry):
        to = pl.ds(pl.multiple_of((mine + t) * rows, rows), rows)
        col_cot[to, :] = cot[t, pl.ds(mine, rows), :].astype(f32)
        return carry

    lax.fori_loop(0, rows, unpack_own, 0)
    for d in range(1, groups):
        cot_copy(d).wait_recv()
    for d in range(1, groups):
        peer = lax.rem(me + d, groups)
        lax.fori_loop(peer * rows, peer * rows + rows, unpack, 0)

    def columns_of(ref, first):
        return jnp.concatenate(
            [ref[pl.ds(first + r, length, stride=rows), :] for r in range(STEP)], axis=0
        ).astype(bf16)

    def col_pass(t, carry):
        first = t * STEP
        _, _, normed = normed_of(columns_of(col_act, first))
        gate = sigmoid(mm(wg_t[...], normed))
        hat, inv = norm_cols(slabs(tri_c, first).astype(bf16).astype(f32))
        cot_t = mm_t(eye[...], columns_of(col_cot, first))
        d_out = mm(wo[...], (cot_t * gate).astype(bf16))
        put_slabs(tri_c, first, norm_back(d_out * out_gain[...], hat, inv))
        return carry

    lax.fori_loop(0, rows // STEP, col_pass, 0)
    sum_second(0, early_bufs)

    def back_cols(h, carry):
        l_all = left[pl.ds(pl.multiple_of(h * length, length), length), :].astype(bf16)
        to = pl.ds(pl.multiple_of(h * rows, rows), rows)
        tri_c[to, :] = mm(tri_c[to, :].astype(bf16), l_all)
        return carry

    lax.fori_loop(0, hidden, back_cols, 0, unroll=8)
    sum_third(0, early_bufs)

    def last_pass(t, carry):
        first = t * STEP
        x = act[pl.ds(first, STEP)].reshape(STEP * length, channels)
        hat, inv, normed = normed_of(x)
        d_proj = half_grad(tri_c, first, mm(w_t[half : 2 * half, :], normed))
        late[:, 0:half] += mm_t(normed, d_proj)
        d_normed = mm(w[:, half : 2 * half], d_proj) + d_normed_sc[t]
        sums[0] += fold(d_normed * hat, length)
        sums[1] += fold(d_normed, length)
        back = norm_back(d_normed * in_gain[...], hat, inv).astype(bf16)
        for r in range(STEP):
            pair_grad[first + r] = mm_t(eye[...], back[:, r * length : (r + 1) * length]).astype(
                bf16
            )
        return carry

    lax.fori_loop(0, rows // STEP, last_pass, 0)

    put_stats(late, 0)
    sum_first(1, late, late_bufs)
    sum_last(0, early_bufs, (gate_grad, out_grad, proj_grad.at[:, 0:half]), out_norm_grad)
    sum_second(1, late_bufs)
    sum_third(1, late_bufs)
    sum_last(1, late_bufs, (proj_grad.at[:, half : 2 * half],), in_norm_grad)

    for s in range(groups):
        low, high = me - s, me + s

        @pl.when((low >= 0) & (me + 1 < groups))
        def _():
            hop(act, low, right_sem, me + 1).wait_send()

        @pl.when((high < groups) & (me >= 1))
        def _():
            hop(act, high, left_sem, me - 1).wait_send()

    for d in range(1, groups):
        cot_copy(d).wait_send()


def shards(
    crops,
    groups,
    pair_act,
    pair_cot,
    in_gain,
    in_bias,
    proj_weight,
    gate_weight,
    out_gain,
    out_bias,
    out_weight,
):
    _, rows, length, channels = pair_act.shape
    hidden = out_weight.shape[0]
    act = pair_act.reshape(rows, length, channels)
    cot = pair_cot.reshape(rows, length, channels)
    vmem = pl.BlockSpec(memory_space=pltpu.VMEM)
    dma = pltpu.SemaphoreType.DMA
    piece = channels // crops

    def sum_bufs(width):
        return tuple(pltpu.VMEM((n, piece, width), f32) for n in (crops, crops, groups, crops))

    early_width, late_width = 3 * channels + 2 * hidden, 2 * hidden + channels
    update, pair_grad, *grads = pl.pallas_call(
        functools.partial(kernel, crops, groups),
        out_shape=(
            jax.ShapeDtypeStruct(act.shape, bf16),
            jax.ShapeDtypeStruct(act.shape, bf16),
            jax.ShapeDtypeStruct(proj_weight.shape, f32),
            jax.ShapeDtypeStruct(gate_weight.shape, f32),
            jax.ShapeDtypeStruct(out_weight.shape, f32),
            jax.ShapeDtypeStruct((2, channels), f32),
            jax.ShapeDtypeStruct((2, hidden), f32),
        ),
        in_specs=[vmem] * 9,
        out_specs=(vmem,) * 7,
        scratch_shapes=[
            pltpu.VMEM((groups, rows, length, channels), bf16),
            pltpu.VMEM((length, rows, channels), bf16),
            pltpu.VMEM((hidden * length, length), f32),
            pltpu.VMEM((hidden * length, length), f32),
            pltpu.VMEM((hidden * rows, length), f32),
            pltpu.VMEM((hidden * rows, length), f32),
            pltpu.VMEM((length * rows, channels), f32),
            pltpu.VMEM((length * rows, channels), f32),
            pltpu.VMEM((rows // STEP, channels, STEP * length), bf16),
            pltpu.VMEM((4, channels, length), f32),
            dma((groups,)),
            dma((groups,)),
            dma((groups,)),
            dma((groups - 1,)),
            dma((groups - 1,)),
            pltpu.VMEM((4 * hidden, channels), bf16),
            pltpu.VMEM((channels, channels), bf16),
            pltpu.VMEM((channels, hidden), bf16),
            pltpu.VMEM((channels, channels), bf16),
            pltpu.VMEM((4, channels, 1), f32),
            pltpu.VMEM((channels, early_width), f32),
            pltpu.VMEM((channels, late_width), f32),
            sum_bufs(early_width),
            sum_bufs(late_width),
            dma((2, 2, 2, crops - 1)),
            dma((2, 2, groups - 1)),
            pltpu.VMEM((rows // STEP, channels, STEP * length), f32),
        ],
        compiler_params=pltpu.CompilerParams(
            collective_id=0, has_side_effects=True, vmem_limit_bytes=60 * 1024 * 1024
        ),
        name="tri",
    )(
        act,
        cot,
        in_gain.reshape(1, channels),
        in_bias.reshape(1, channels),
        proj_weight,
        gate_weight,
        out_gain.reshape(1, hidden),
        out_bias.reshape(1, hidden),
        out_weight,
    )
    return (update.reshape(pair_act.shape), pair_grad.reshape(pair_act.shape), *grads)


def solution(mesh):
    placed = (P("dp", "dap", None, None),) * 2 + (P(),) * 7
    return jax.shard_map(
        functools.partial(shards, mesh.shape["dp"], mesh.shape["dap"]),
        mesh=mesh,
        in_specs=placed,
        out_specs=(P("dp", "dap", None, None), P("dp", "dap", None, None), P(), P(), P(), P(), P()),
        check_vma=False,
    )
```

```python
import functools

import jax
import jax.numpy as jnp
from jax import lax
from jax.experimental import pallas as pl
from jax.experimental.pallas import tpu as pltpu
from jax.sharding import PartitionSpec as P

epsilon = 1e-05
f32 = jnp.float32
bf16 = jnp.bfloat16
STEP = 8
CUTS = 2


def mm(a, b):
    return jnp.dot(a, b, preferred_element_type=f32)


def mm_t(a, b):
    return lax.dot_general(a, b, (((1,), (1,)), ((), ())), preferred_element_type=f32)


def sigmoid(v):
    return 0.5 * jnp.tanh(0.5 * v) + 0.5


def norm_cols(values):
    count = values.shape[0]
    centred = values - jnp.sum(values, axis=0, keepdims=True) * (1.0 / count)
    var = jnp.sum(centred * centred, axis=0, keepdims=True) * (1.0 / count)
    inv_std = lax.rsqrt(var + epsilon)
    return centred * inv_std, inv_std


def norm_back(grad_hat, x_hat, inv_std):
    count = grad_hat.shape[0]
    first = jnp.sum(grad_hat, axis=0, keepdims=True) * (1.0 / count)
    second = jnp.sum(grad_hat * x_hat, axis=0, keepdims=True) * (1.0 / count)
    return (grad_hat - first - x_hat * second) * inv_std


def fold(values, width):
    total = values[:, 0:width]
    for at in range(width, values.shape[1], width):
        total = total + values[:, at : at + width]
    return total


def kernel(
    crops,
    groups,
    act,
    cot,
    in_gain_row,
    in_bias_row,
    w,
    wg,
    out_gain_row,
    out_bias_row,
    wo,
    update,
    pair_grad,
    proj_grad,
    gate_grad,
    out_grad,
    in_norm_grad,
    out_norm_grad,
    act_all,
    cot_cols,
    left,
    right,
    tri_r,
    tri_c,
    col_act,
    col_cot,
    d_gate_sc,
    sums,
    recv_sem,
    right_sem,
    left_sem,
    cot_send,
    cot_recv,
    w_t,
    wg_t,
    wo_t,
    eye,
    columns,
    early,
    late,
    early_bufs,
    late_bufs,
    sum_sems,
    swap_sems,
    d_normed_sc,
):
    me = lax.axis_index("dap")
    crop = lax.axis_index("dp")
    rows, length, channels = act.shape
    hidden = wo.shape[0]

    barrier = pltpu.get_barrier_semaphore()
    for d in range(1, groups):
        pl.semaphore_signal(
            barrier,
            inc=1,
            device_id={"dap": lax.rem(me + d, groups)},
            device_id_type=pl.DeviceIdType.MESH,
        )
    for d in range(1, crops):
        pl.semaphore_signal(
            barrier,
            inc=1,
            device_id={"dp": lax.rem(crop + d, crops)},
            device_id_type=pl.DeviceIdType.MESH,
        )
    pl.semaphore_wait(barrier, groups + crops - 2)

    cut = rows // CUTS

    def hop(src, block, c, send_sems, to):
        part = pl.ds(c * cut, cut)
        return pltpu.make_async_remote_copy(
            src_ref=src.at[part],
            dst_ref=act_all.at[block, part],
            send_sem=send_sems.at[block, c],
            recv_sem=recv_sem.at[block, c],
            device_id={"dap": to},
            device_id_type=pl.DeviceIdType.MESH,
        )

    def cot_copy(d):
        peer = lax.rem(me + d, groups)
        at = pl.multiple_of(peer * rows, rows)
        mine = pl.multiple_of(me * rows, rows)
        return pltpu.make_async_remote_copy(
            src_ref=cot.at[:, pl.ds(at, rows), :],
            dst_ref=cot_cols.at[pl.ds(mine, rows)],
            send_sem=cot_send.at[d - 1],
            recv_sem=cot_recv.at[d - 1],
            device_id={"dap": peer},
            device_id_type=pl.DeviceIdType.MESH,
        )

    @pl.when(me + 1 < groups)
    def _():
        for c in range(CUTS):
            hop(act, me, c, right_sem, me + 1).start()

    @pl.when(me >= 1)
    def _():
        for c in range(CUTS):
            hop(act, me, c, left_sem, me - 1).start()

    def turned(block):
        return jnp.transpose(block.astype(f32)).astype(bf16)

    for n in range(4):
        w_t[n * hidden : (n + 1) * hidden, :] = turned(w[:, n * hidden : (n + 1) * hidden])
    wg_t[...] = turned(wg[...])
    wo_t[...] = turned(wo[...])
    square = (channels, channels)
    eye[...] = (
        (lax.broadcasted_iota(jnp.int32, square, 0) == lax.broadcasted_iota(jnp.int32, square, 1))
        .astype(f32)
        .astype(bf16)
    )
    for n, row in enumerate((in_gain_row, in_bias_row, out_gain_row, out_bias_row)):
        columns[n] = jnp.transpose(jnp.broadcast_to(row[...], square))[:, 0:1]
    in_gain, in_bias, out_gain, out_bias = (columns.at[n] for n in range(4))

    def piece_copy(which, stage, bufs, e):
        peer = lax.rem(crop + e, crops)
        sent, got, _, total = bufs
        src, dst = (sent.at[peer], got.at[crop]) if stage == 0 else (total.at[crop],) * 2
        return pltpu.make_async_remote_copy(
            src_ref=src,
            dst_ref=dst,
            send_sem=sum_sems.at[which, stage, 0, e - 1],
            recv_sem=sum_sems.at[which, stage, 1, e - 1],
            device_id={"dp": peer},
            device_id_type=pl.DeviceIdType.MESH,
        )

    def swap_copy(which, bufs, d):
        part = bufs[2]
        return pltpu.make_async_remote_copy(
            src_ref=part.at[me],
            dst_ref=part.at[me],
            send_sem=swap_sems.at[which, 0, d - 1],
            recv_sem=swap_sems.at[which, 1, d - 1],
            device_id={"dap": lax.rem(me + d, groups)},
            device_id_type=pl.DeviceIdType.MESH,
        )

    piece = channels // crops

    def sum_first(which, acc, bufs):
        for p in range(crops):
            bufs[0][p] = acc[p * piece : (p + 1) * piece, :]
        for e in range(1, crops):
            piece_copy(which, 0, bufs, e).start()

    def sum_second(which, bufs):
        total = bufs[0][crop]
        for e in range(1, crops):
            piece_copy(which, 0, bufs, e).wait_recv()
            total = total + bufs[1][lax.rem(crop + crops - e, crops)]
        bufs[2][me] = total
        for d in range(1, groups):
            swap_copy(which, bufs, d).start()

    def sum_third(which, bufs):
        for d in range(1, groups):
            swap_copy(which, bufs, d).wait_recv()
        total = bufs[2][0]
        for g in range(1, groups):
            total = total + bufs[2][g]
        bufs[3][crop] = total * (1.0 / length)
        for e in range(1, crops):
            piece_copy(which, 1, bufs, e).start()

    def sum_last(which, bufs, outs, stats_out):
        for e in range(1, crops):
            piece_copy(which, 1, bufs, e).wait_recv()
        total = jnp.concatenate([bufs[3][p] for p in range(crops)], axis=0)
        at = 0
        for out in outs:
            out[...] = total[:, at : at + out.shape[1]]
            at += out.shape[1]
        turned_stats = jnp.transpose(total[:, at : at + channels])
        stats_out[0:1, :] = turned_stats[0:1]
        stats_out[1:2, :] = turned_stats[8:9]
        for e in range(1, crops):
            piece_copy(which, 0, bufs, e).wait_send()
            piece_copy(which, 1, bufs, e).wait_send()
        for d in range(1, groups):
            swap_copy(which, bufs, d).wait_send()

    def put_stats(acc, first):
        at = acc.shape[1] - channels
        for n in range(2):
            acc[:, at + 8 * n : at + 8 * n + 8] = jnp.broadcast_to(
                jnp.sum(sums[first + n], axis=1, keepdims=True), (channels, 8)
            )

    def normed_of(x):
        hat, inv = norm_cols(mm_t(eye[...], x))
        return hat, inv, (hat * in_gain[...] + in_bias[...]).astype(bf16)

    def sides(src, base, start, count):
        def body(t, carry):
            x = src[pl.ds(t * STEP, STEP)].reshape(STEP * length, channels)
            _, _, normed = normed_of(x)
            pj = mm(w_t[...], normed)
            lv = sigmoid(pj[0:hidden]) * pj[hidden : 2 * hidden]
            rv = sigmoid(pj[2 * hidden : 3 * hidden]) * pj[3 * hidden : 4 * hidden]
            for r in range(STEP):
                row = base + t * STEP + r
                lanes = slice(r * length, (r + 1) * length)
                left[pl.ds(row, hidden, stride=length), :] = lv[:, lanes]
                right[pl.ds(row, hidden, stride=length), :] = rv[:, lanes]
                own = src[t * STEP + r, pl.ds(pl.multiple_of(me * rows, rows), rows), :]
                col_act[pl.ds(pl.multiple_of(row * rows, rows), rows), :] = own.astype(f32)
            return carry

        lax.fori_loop(start // STEP, (start + count) // STEP, body, 0)

    sides(act, me * rows, 0, rows)
    for s in range(1, groups):
        low, high = me - s, me + s
        for c in range(CUTS):

            @pl.when(low >= 0)
            def _():
                hop(act, low, c, right_sem, me).wait_recv()

                @pl.when(me + 1 < groups)
                def _():
                    hop(act_all.at[low], low, c, right_sem, me + 1).start()

            @pl.when(high < groups)
            def _():
                hop(act, high, c, left_sem, me).wait_recv()

                @pl.when(me >= 1)
                def _():
                    hop(act_all.at[high], high, c, left_sem, me - 1).start()

            if s == groups - 1 and c == CUTS - 1:
                for d in range(1, groups):
                    cot_copy(d).start()

            @pl.when(low >= 0)
            def _():
                sides(act_all.at[low], low * rows, c * cut, cut)

            @pl.when(high < groups)
            def _():
                sides(act_all.at[high], high * rows, c * cut, cut)

    mine = pl.multiple_of(me * rows, rows)

    def products(h, carry):
        at = pl.multiple_of(h * length, length)
        l_all = left[pl.ds(at, length), :].astype(bf16)
        r_all = right[pl.ds(at, length), :].astype(bf16)
        l_own = left[pl.ds(pl.multiple_of(at + mine, rows), rows), :].astype(bf16)
        r_own = right[pl.ds(pl.multiple_of(at + mine, rows), rows), :].astype(bf16)
        to = pl.ds(pl.multiple_of(h * rows, rows), rows)
        tri_r[to, :] = mm_t(l_own, r_all)
        tri_c[to, :] = mm_t(r_own, l_all)
        return carry

    lax.fori_loop(0, hidden, products, 0, unroll=4)

    def slabs(ref, first):
        return jnp.concatenate(
            [ref[pl.ds(first + r, hidden, stride=rows), :] for r in range(STEP)], axis=1
        )

    def put_slabs(ref, first, values):
        for r in range(STEP):
            ref[pl.ds(first + r, hidden, stride=rows), :] = values[
                :, r * length : (r + 1) * length
            ]

    sums[...] = jnp.zeros_like(sums)
    early[...] = jnp.zeros_like(early)
    late[...] = jnp.zeros_like(late)

    def row_pass(t, carry):
        first = t * STEP
        x = act[pl.ds(first, STEP)].reshape(STEP * length, channels)
        _, _, normed = normed_of(x)
        gate = sigmoid(mm(wg_t[...], normed))
        hat, inv = norm_cols(slabs(tri_r, first).astype(bf16).astype(f32))
        tri_norm = (hat * out_gain[...] + out_bias[...]).astype(bf16)
        mixed = mm(wo_t[...], tri_norm)
        upd = (gate * mixed).astype(bf16)
        for r in range(STEP):
            update[first + r] = mm_t(eye[...], upd[:, r * length : (r + 1) * length]).astype(bf16)
        cot_t = mm_t(eye[...], cot[pl.ds(first, STEP)].reshape(STEP * length, channels))
        d_mixed_f = cot_t * gate
        d_mixed = d_mixed_f.astype(bf16)
        d_gate = (d_mixed_f * mixed * (1.0 - gate)).astype(bf16)
        d_gate_sc[t] = d_gate
        early[:, 0:channels] += mm_t(normed, d_gate)
        early[:, channels : 2 * channels] += mm_t(tri_norm, d_mixed)
        d_out = mm(wo[...], d_mixed)
        sums[2] += fold(d_out * hat, length)
        sums[3] += fold(d_out, length)
        put_slabs(tri_r, first, norm_back(d_out * out_gain[...], hat, inv))
        return carry

    lax.fori_loop(0, rows // STEP, row_pass, 0)

    def back_rows(h, carry):
        r_all = right[pl.ds(pl.multiple_of(h * length, length), length), :].astype(bf16)
        to = pl.ds(pl.multiple_of(h * rows, rows), rows)
        tri_r[to, :] = mm(tri_r[to, :].astype(bf16), r_all)
        return carry

    lax.fori_loop(0, hidden, back_rows, 0, unroll=8)

    half = 2 * hidden

    def half_grad(ref, first, pj):
        grad = slabs(ref, first).astype(bf16).astype(f32)
        sg = sigmoid(pj[0:hidden])
        d_val = grad * sg
        d_pre = d_val * pj[hidden:half] * (1.0 - sg)
        return jnp.concatenate([d_pre.astype(bf16), d_val.astype(bf16)], axis=0)

    def left_pass(t, carry):
        first = t * STEP
        x = act[pl.ds(first, STEP)].reshape(STEP * length, channels)
        _, _, normed = normed_of(x)
        d_proj = half_grad(tri_r, first, mm(w_t[0:half, :], normed))
        early[:, 2 * channels : 2 * channels + half] += mm_t(normed, d_proj)
        d_normed_sc[t] = mm(w[:, 0:half], d_proj) + mm(wg[...], d_gate_sc[t])
        return carry

    lax.fori_loop(0, rows // STEP, left_pass, 0)
    put_stats(early, 2)
    sum_first(0, early, early_bufs)

    def unpack(t, carry):
        to = pl.ds(pl.multiple_of(t * rows, rows), rows)
        col_cot[to, :] = cot_cols[t].astype(f32)
        return carry

    def unpack_own(t, carry):
        to = pl.ds(pl.multiple_of((mine + t) * rows, rows), rows)
        col_cot[to, :] = cot[t, pl.ds(mine, rows), :].astype(f32)
        return carry

    lax.fori_loop(0, rows, unpack_own, 0)
    for d in range(1, groups):
        cot_copy(d).wait_recv()
    for d in range(1, groups):
        peer = lax.rem(me + d, groups)
        lax.fori_loop(peer * rows, peer * rows + rows, unpack, 0)

    def columns_of(ref, first):
        return jnp.concatenate(
            [ref[pl.ds(first + r, length, stride=rows), :] for r in range(STEP)], axis=0
        ).astype(bf16)

    def col_pass(t, carry):
        first = t * STEP
        _, _, normed = normed_of(columns_of(col_act, first))
        gate = sigmoid(mm(wg_t[...], normed))
        hat, inv = norm_cols(slabs(tri_c, first).astype(bf16).astype(f32))
        cot_t = mm_t(eye[...], columns_of(col_cot, first))
        d_out = mm(wo[...], (cot_t * gate).astype(bf16))
        put_slabs(tri_c, first, norm_back(d_out * out_gain[...], hat, inv))
        return carry

    lax.fori_loop(0, rows // STEP, col_pass, 0)
    sum_second(0, early_bufs)

    def back_cols(h, carry):
        l_all = left[pl.ds(pl.multiple_of(h * length, length), length), :].astype(bf16)
        to = pl.ds(pl.multiple_of(h * rows, rows), rows)
        tri_c[to, :] = mm(tri_c[to, :].astype(bf16), l_all)
        return carry

    lax.fori_loop(0, hidden, back_cols, 0, unroll=8)
    sum_third(0, early_bufs)

    def last_pass(t, carry):
        first = t * STEP
        x = act[pl.ds(first, STEP)].reshape(STEP * length, channels)
        hat, inv, normed = normed_of(x)
        d_proj = half_grad(tri_c, first, mm(w_t[half : 2 * half, :], normed))
        late[:, 0:half] += mm_t(normed, d_proj)
        d_normed = mm(w[:, half : 2 * half], d_proj) + d_normed_sc[t]
        sums[0] += fold(d_normed * hat, length)
        sums[1] += fold(d_normed, length)
        back = norm_back(d_normed * in_gain[...], hat, inv).astype(bf16)
        for r in range(STEP):
            pair_grad[first + r] = mm_t(eye[...], back[:, r * length : (r + 1) * length]).astype(
                bf16
            )
        return carry

    lax.fori_loop(0, rows // STEP, last_pass, 0)

    put_stats(late, 0)
    sum_first(1, late, late_bufs)
    sum_last(0, early_bufs, (gate_grad, out_grad, proj_grad.at[:, 0:half]), out_norm_grad)
    sum_second(1, late_bufs)
    sum_third(1, late_bufs)
    sum_last(1, late_bufs, (proj_grad.at[:, half : 2 * half],), in_norm_grad)

    for s in range(groups):
        low, high = me - s, me + s

        @pl.when((low >= 0) & (me + 1 < groups))
        def _():
            for c in range(CUTS):
                hop(act, low, c, right_sem, me + 1).wait_send()

        @pl.when((high < groups) & (me >= 1))
        def _():
            for c in range(CUTS):
                hop(act, high, c, left_sem, me - 1).wait_send()

    for d in range(1, groups):
        cot_copy(d).wait_send()


def shards(
    crops,
    groups,
    pair_act,
    pair_cot,
    in_gain,
    in_bias,
    proj_weight,
    gate_weight,
    out_gain,
    out_bias,
    out_weight,
):
    _, rows, length, channels = pair_act.shape
    hidden = out_weight.shape[0]
    act = pair_act.reshape(rows, length, channels)
    cot = pair_cot.reshape(rows, length, channels)
    vmem = pl.BlockSpec(memory_space=pltpu.VMEM)
    dma = pltpu.SemaphoreType.DMA
    piece = channels // crops

    def sum_bufs(width):
        return tuple(pltpu.VMEM((n, piece, width), f32) for n in (crops, crops, groups, crops))

    early_width, late_width = 3 * channels + 2 * hidden, 2 * hidden + channels
    update, pair_grad, *grads = pl.pallas_call(
        functools.partial(kernel, crops, groups),
        out_shape=(
            jax.ShapeDtypeStruct(act.shape, bf16),
            jax.ShapeDtypeStruct(act.shape, bf16),
            jax.ShapeDtypeStruct(proj_weight.shape, f32),
            jax.ShapeDtypeStruct(gate_weight.shape, f32),
            jax.ShapeDtypeStruct(out_weight.shape, f32),
            jax.ShapeDtypeStruct((2, channels), f32),
            jax.ShapeDtypeStruct((2, hidden), f32),
        ),
        in_specs=[vmem] * 9,
        out_specs=(vmem,) * 7,
        scratch_shapes=[
            pltpu.VMEM((groups, rows, length, channels), bf16),
            pltpu.VMEM((length, rows, channels), bf16),
            pltpu.VMEM((hidden * length, length), f32),
            pltpu.VMEM((hidden * length, length), f32),
            pltpu.VMEM((hidden * rows, length), f32),
            pltpu.VMEM((hidden * rows, length), f32),
            pltpu.VMEM((length * rows, channels), f32),
            pltpu.VMEM((length * rows, channels), f32),
            pltpu.VMEM((rows // STEP, channels, STEP * length), bf16),
            pltpu.VMEM((4, channels, length), f32),
            dma((groups, CUTS)),
            dma((groups, CUTS)),
            dma((groups, CUTS)),
            dma((groups - 1,)),
            dma((groups - 1,)),
            pltpu.VMEM((4 * hidden, channels), bf16),
            pltpu.VMEM((channels, channels), bf16),
            pltpu.VMEM((channels, hidden), bf16),
            pltpu.VMEM((channels, channels), bf16),
            pltpu.VMEM((4, channels, 1), f32),
            pltpu.VMEM((channels, early_width), f32),
            pltpu.VMEM((channels, late_width), f32),
            sum_bufs(early_width),
            sum_bufs(late_width),
            dma((2, 2, 2, crops - 1)),
            dma((2, 2, groups - 1)),
            pltpu.VMEM((rows // STEP, channels, STEP * length), f32),
        ],
        compiler_params=pltpu.CompilerParams(
            collective_id=0, has_side_effects=True, vmem_limit_bytes=60 * 1024 * 1024
        ),
        name="tri",
    )(
        act,
        cot,
        in_gain.reshape(1, channels),
        in_bias.reshape(1, channels),
        proj_weight,
        gate_weight,
        out_gain.reshape(1, hidden),
        out_bias.reshape(1, hidden),
        out_weight,
    )
    return (update.reshape(pair_act.shape), pair_grad.reshape(pair_act.shape), *grads)


def solution(mesh):
    placed = (P("dp", "dap", None, None),) * 2 + (P(),) * 7
    return jax.shard_map(
        functools.partial(shards, mesh.shape["dp"], mesh.shape["dap"]),
        mesh=mesh,
        in_specs=placed,
        out_specs=(P("dp", "dap", None, None), P("dp", "dap", None, None), P(), P(), P(), P(), P()),
        check_vma=False,
    )
```
